128 devices in a mesh: chan: 32 (over x, y, core), int: 4 (over z).
Axes of the slice: x: 4, y: 4, z: 4, core: 2. Of those that a mesh axis runs over, the one named last changes fastest.
Arguments:
- t_pp: bfloat16 [131072, 2048], P(('chan', 'int')), may hold values from -6 to 6
- interaction: bfloat16 [4, 2048, 2048], P(None, None, 'int'), may hold values from -0.125 to 0.125
- send_order: int32 [131072], P(('chan', 'int')), may hold values from 0 to 1023, as said below
- recv_order: int32 [131072], P(('chan', 'int')), may hold values from 0 to 1023, as said below
- ph_channel: int32 [131072], P('chan'), may hold values from 0 to 4, as said below
- recouple_weight: float32 [131072], P('chan'), may hold values from -1.5 to 1.5
Outputs:
- term_pp: bfloat16 [131072, 2048], P(('chan', 'int'))
The draws below stay inside these ranges and needn't reach their ends.
Inputs may be any that keep to these rules, and one draw needn't show every extreme that they name: `send_order`: within each device's 1024 slots a permutation of its local rows. `recv_order`: within each device's 1024 slots a permutation of its received rows. `ph_channel`: non-decreasing within each device's 1024 slots; the value 4 marks empty slots, which come last; some device has no empty slot.
All inputs are finite; a program needn't handle non-finite values.
Results may differ from the reference program's by a relative error of at most 0.001.
Values may be sent and summed in bfloat16 or wider, within the bound.
A program may use at most 128 MiB of HBM per device.

```python
import jax
import jax.numpy as jnp
from jax import lax

W = 2048
NCH = 4
R_DEV = 1024
ROWS = 131072
N_CHAN = 32
N_INT = 4


def draw_send_order(key, part):
    block_count = ROWS // R_DEV
    keys = jax.random.split(jax.random.fold_in(key, 3), block_count)
    perms = jax.vmap(lambda one_key: jax.random.permutation(one_key, R_DEV))(keys)
    return perms.reshape(ROWS).astype(jnp.int32)


def draw_recv_order(key, part):
    block_count = ROWS // R_DEV
    keys = jax.random.split(jax.random.fold_in(key, 7), block_count)
    perms = jax.vmap(lambda one_key: jax.random.permutation(one_key, R_DEV))(keys)
    return perms.reshape(ROWS).astype(jnp.int32)


def draw_ph_channel(key, part):
    block_count = ROWS // R_DEV
    first_key, second_key, third_key = jax.random.split(jax.random.fold_in(key, 11), 3)
    live = jax.random.randint(first_key, (block_count,), R_DEV // 4, R_DEV + 1)
    full_block = jax.random.randint(second_key, (), 0, block_count)
    live = jnp.where(jnp.arange(block_count) == full_block, R_DEV, live)
    cuts = jax.random.randint(third_key, (block_count, NCH - 1), 0, R_DEV + 1)
    cuts = jnp.minimum(cuts, live[:, None])
    slots = jnp.arange(R_DEV)
    channel_ids = jnp.sum((cuts[:, None, :] <= slots[None, :, None]).astype(jnp.int32), axis=2)
    channel_ids = jnp.where(slots[None, :] < live[:, None], channel_ids, NCH)
    return channel_ids.reshape(ROWS).astype(jnp.int32)


def level_of(rng, shape, cuts, least, top_value):
    def one(dim, blocks):
        draws = jax.random.uniform(jax.random.fold_in(jax.random.fold_in(rng, 6), dim), (blocks,), jnp.float32, least / len(cuts), top_value / len(cuts))
        return jnp.repeat(jnp.exp(draws), shape[dim] // blocks).reshape((-1,) + (1,) * (len(shape) - dim - 1))

    gain = one(*cuts[0])
    for cut in cuts[1:]:
        gain = gain * one(*cut)
    return gain


def normal_values(key, dims, width, reach, cuts=(), held_as=jnp.bfloat16):
    values = jax.random.normal(key, dims, jnp.float32) * width
    if len(cuts) > 0:
        values = level_of(key, dims, cuts, -0.22, 0.18) * values
    return jnp.clip(values, min=-reach, max=reach).astype(held_as)


def setup_inputs(seed: int = 0) -> dict:
    arg_keys = jax.random.split(jax.random.key(seed), 7)
    return {
        "t_pp": normal_values(arg_keys[0], (ROWS, W), 1.0, 6.0, ((0, 128),)),
        "interaction": normal_values(arg_keys[1], (NCH, W, W), W ** -0.5, 0.125, ((2, 4),)),
        "send_order": draw_send_order(jax.random.fold_in(arg_keys[6], 71), 0),
        "recv_order": draw_recv_order(jax.random.fold_in(arg_keys[6], 71), 0),
        "ph_channel": draw_ph_channel(jax.random.fold_in(arg_keys[6], 71), 0),
        "recouple_weight": jnp.clip(jax.random.uniform(arg_keys[5], (ROWS,), jnp.float32, -1.5, 1.5) * level_of(arg_keys[5], (ROWS,), ((0, 32),), -0.4, 0.0), -1.5, 1.5),
    }


def reference(t_pp, interaction, send_order, recv_order, ph_channel, recouple_weight):
    quota = R_DEV // N_CHAN
    block_count = N_CHAN * N_INT
    position = jnp.arange(ROWS, dtype=jnp.int32)
    block_index = position // R_DEV
    arrived = recv_order.astype(jnp.int32)
    target_chan = block_index // N_INT
    int_index = block_index % N_INT
    source_block = (arrived // quota) * N_INT + int_index
    source_slot = target_chan * quota + arrived % quota
    source = (source_block * R_DEV + send_order[source_block * R_DEV + source_slot]).astype(jnp.int32)
    t_ph = t_pp[source].reshape(block_count, R_DEV, W)
    channel_ids = ph_channel.reshape(block_count, R_DEV)
    weights = recouple_weight.reshape(block_count, R_DEV)

    def one_block(packed):
        amps, ids, scale = packed
        total = jnp.zeros((R_DEV, W), jnp.float32)
        for channel in range(NCH):
            product = jnp.dot(amps, interaction[channel], preferred_element_type=jnp.float32)
            total = total + jnp.where((ids == channel)[:, None], product, jnp.float32(0.0))
        result = jnp.where((ids < NCH)[:, None], scale[:, None] * total, jnp.float32(0.0))
        return result.astype(jnp.bfloat16)

    z_ph = lax.map(one_block, (t_ph, channel_ids, weights)).reshape(ROWS, W)
    return jnp.zeros((ROWS, W), jnp.bfloat16).at[source].set(z_ph)
```

```python
import jax
import jax.numpy as jnp
from jax import lax
from jax.experimental import pallas as pl
from jax.experimental.pallas import tpu as pltpu
from jax.sharding import PartitionSpec as P

NX, NY, NCORE, NZ = 4, 4, 2, 4
G = 4
MT = 512
BF = jnp.bfloat16
F32 = jnp.float32


def spread(position, values):
    hit = position[None, :] == jnp.arange(position.shape[0], dtype=jnp.int32)[:, None]
    return [jnp.sum(jnp.where(hit, v[None, :], jnp.float32(0.0)), axis=1) for v in values]


def kernel(t_hbm, w_hbm, ch_ref, scale_ref, out_hbm, wbuf, tm, tbuf, acc, local_sem, out_sem, send_sem, recv_sem):
    rows, width = t_hbm.shape
    chan = lax.axis_index("chan")
    z = lax.axis_index("int")
    core = chan % NCORE
    y = (chan // NCORE) % NY
    x = chan // (NCORE * NY)

    def at_xy(px, py, pc):
        return {"chan": (px * NY + py) * NCORE + pc}

    xp, xm = at_xy((x + 1) % NX, y, core), at_xy((x + NX - 1) % NX, y, core)
    yp, ym = at_xy(x, (y + 1) % NY, core), at_xy(x, (y + NY - 1) % NY, core)
    zp, zm = {"int": (z + 1) % NZ}, {"int": (z + NZ - 1) % NZ}
    sib = at_xy(x, y, 1 - core)
    links = (xp, xm, yp, ym, zp, zm, sib)
    XP, XM, YP, YM, ZP, ZM, SIB = range(7)
    steps = 3 * G

    t_copy = pltpu.make_async_copy(t_hbm, tbuf, local_sem.at[G])
    t_copy.start()
    for g in range(G):
        for c in range(4):
            pltpu.make_async_copy(w_hbm.at[c, :, g], wbuf.at[pl.ds(g * 16 + c * 4, 4)], local_sem.at[g]).start()

    barrier = pltpu.get_barrier_semaphore()
    for peer in links:
        pl.semaphore_signal(barrier, inc=1, device_id=peer, device_id_type=pl.DeviceIdType.MESH)
    pl.semaphore_wait(barrier, 7)

    def spot(dq, g, c, kq):
        return ((dq * G + g) * 4 + c) * 4 + kq

    def send(link, src, dst_index):
        pltpu.make_async_remote_copy(
            src_ref=src,
            dst_ref=wbuf.at[dst_index],
            send_sem=send_sem.at[link],
            recv_sem=recv_sem.at[dst_index - G * 16],
            device_id=links[link],
            device_id_type=pl.DeviceIdType.MESH,
        ).start()

    def forward(link, index):
        send(link, wbuf.at[index], index)

    def arrive(index):
        pltpu.make_async_copy(wbuf.at[index], wbuf.at[index], recv_sem.at[index - G * 16]).wait()

    cx, cy = 2 * core, 2 * core + 1

    for g in range(G):
        for c, kq in ((cx, x), (cy, y)):
            src = w_hbm.at[c, kq, g]
            send(ZP, src, spot(3, g, c, kq))
            send(ZM, src, spot(1, g, c, kq))

    t_copy.wait()
    for c in range(4):
        @pl.loop(0, rows // 128)
        def _(m):
            r = pl.multiple_of(m * 128, 128)
            keep = (ch_ref[pl.ds(r, 128), :] == jnp.float32(c))
            for g in range(G):
                for kq in range(4):
                    col = (kq * G + g) * 128
                    v = tbuf[pl.ds(r, 128), col : col + 128]
                    tm[g, pl.ds(r, 128), (c * 4 + kq) * 128 : (c * 4 + kq + 1) * 128] = jnp.where(
                        keep, v.astype(F32), jnp.float32(0.0)
                    ).astype(BF)

    def place(s):
        early = 1 - s // (2 * G)
        dq = early * (1 + 2 * (s % 2)) + (1 - early) * 2
        g = early * (s // 2) + (1 - early) * (s - 2 * G)
        return dq, g

    def unit(dq, g, slot):
        @pl.loop(0, rows // MT)
        def _(m):
            r = pl.ds(pl.multiple_of(m * MT, MT), MT)

            @pl.when(g == 0)
            def _():
                acc[slot, r, :] = jnp.zeros((MT, 512), F32)

            rhs = wbuf[pl.ds((dq * G + g) * 16, 16)].reshape(2048, 512)
            acc[slot, r, :] += jnp.dot(tm[g, r, :], rhs, preferred_element_type=F32)

        @pl.when(g == G - 1)
        def _():
            col = pl.ds(pl.multiple_of(((z + dq) % NZ) * 512, 512), 512)

            @pl.loop(0, rows // 128)
            def _(m):
                r = pl.ds(pl.multiple_of(m * 128, 128), 128)
                sc = scale_ref[r, :]
                for part in range(4):
                    lanes = pl.ds(pl.multiple_of(((z + dq) % NZ) * 512 + part * 128, 128), 128)
                    tbuf[r, lanes] = (acc[slot, r, part * 128 : (part + 1) * 128] * sc).astype(BF)

            pltpu.make_async_copy(tbuf.at[:, col], out_hbm.at[:, col], out_sem.at[dq]).start()

    def step(s, carry):
        @pl.when(s < steps)
        def _():
            dq, g = place(s)
            for c, kq, plus, minus in ((cx, x, XP, XM), (cy, y, YP, YM)):
                index = spot(dq, g, c, kq)
                arrive(index)
                forward(plus, index)
                forward(minus, index)
                forward(SIB, index)

            @pl.when(dq == 3)
            def _():
                send(ZP, wbuf.at[spot(3, g, cx, x)], spot(2, g, cx, x))

            @pl.when(dq == 1)
            def _():
                send(ZM, wbuf.at[spot(1, g, cy, y)], spot(2, g, cy, y))

        @pl.when(jnp.logical_and(s >= 1, s < steps + 1))
        def _():
            dq, g = place(s - 1)
            for c, kq, plus, minus in ((cx, x, XP, XM), (cy, y, YP, YM)):
                below, above = spot(dq, g, c, (kq + 3) % 4), spot(dq, g, c, (kq + 1) % 4)
                arrive(below)
                arrive(above)

                @pl.when(g < G // 2)
                def _():
                    forward(plus, below)

                @pl.when(g >= G // 2)
                def _():
                    forward(minus, above)

                forward(SIB, below)
                forward(SIB, above)

        @pl.when(s < G)
        def _():
            pltpu.make_async_copy(wbuf.at[pl.ds(s * 16, 16)], wbuf.at[pl.ds(s * 16, 16)], local_sem.at[s]).wait()
            unit(0, s, 1)

        @pl.when(s >= 3)
        def _():
            dq, g = place(s - 3)
            for c in (2 - 2 * core, 3 - 2 * core):
                for kq in range(4):
                    arrive(spot(dq, g, c, kq))
            unit(dq, g, dq - 1)

        @pl.when(jnp.logical_and(s >= 2, s < steps + 2))
        def _():
            dq, g = place(s - 2)
            for c, kq in ((cx, x), (cy, y)):
                index = spot(dq, g, c, (kq + 2) % 4)
                arrive(index)
                forward(SIB, index)

        return carry

    lax.fori_loop(0, steps + 3, step, 0)

    for link, count in ((XP, 18), (XM, 18), (YP, 18), (YM, 18), (ZP, 12), (ZM, 12), (SIB, 96)):
        whole = wbuf.at[pl.ds(0, count)]
        pltpu.make_async_copy(whole, whole, send_sem.at[link]).wait()
    for dq in range(4):
        part = pl.ds(0, 512)
        pltpu.make_async_copy(tbuf.at[:, part], out_hbm.at[:, part], out_sem.at[dq]).wait()


def on_device(t_pp, interaction, send_order, recv_order, ph_channel, recouple_weight):
    rows = t_pp.shape[0]
    n_chan = lax.axis_size("chan")
    quota = rows // n_chan
    start = lax.axis_index("int") * rows
    ids = lax.dynamic_slice(ph_channel, (start,), (rows,)).astype(F32)
    scale = lax.dynamic_slice(recouple_weight, (start,), (rows,))
    ids_r, scale_r = spread(recv_order, [ids, scale])
    packed = jnp.stack([ids_r.reshape(n_chan, quota), scale_r.reshape(n_chan, quota)], axis=1)
    packed = lax.all_to_all(packed, "chan", split_axis=0, concat_axis=0, tiled=True)
    ids_u, scale_u = packed[:, 0].reshape(rows), packed[:, 1].reshape(rows)
    ids_p, scale_p = spread(send_order, [ids_u, scale_u])
    ids_p = jnp.broadcast_to(ids_p[:, None], (rows, 128))
    scale_p = jnp.broadcast_to(scale_p[:, None], (rows, 128))
    pieces = interaction.reshape(4, 4, G, 128, 512)
    anyspace = pl.BlockSpec(memory_space=pl.ANY)
    vmem = pl.BlockSpec(memory_space=pltpu.VMEM)
    return pl.pallas_call(
        kernel,
        out_shape=jax.ShapeDtypeStruct(t_pp.shape, BF),
        in_specs=[anyspace, anyspace, vmem, vmem],
        out_specs=anyspace,
        scratch_shapes=[
            pltpu.VMEM((4 * G * 16, 128, 512), BF),
            pltpu.VMEM((G, rows, 2048), BF),
            pltpu.VMEM((rows, 2048), BF),
            pltpu.VMEM((3, rows, 512), F32),
            pltpu.SemaphoreType.DMA((G + 1,)),
            pltpu.SemaphoreType.DMA((4,)),
            pltpu.SemaphoreType.DMA((7,)),
            pltpu.SemaphoreType.DMA((3 * G * 16,)),
        ],
        compiler_params=pltpu.CompilerParams(
            collective_id=0, has_side_effects=True, vmem_limit_bytes=66 * 1000 * 1000
        ),
    )(t_pp, pieces, ids_p, scale_p)


def solution(mesh):
    in_specs = (
        P(("chan", "int"), None),
        P(None, None, "int"),
        P(("chan", "int")),
        P(("chan", "int")),
        P("chan"),
        P("chan"),
    )
    out_specs = P(("chan", "int"), None)
    return jax.shard_map(
        on_device, mesh=mesh, in_specs=in_specs, out_specs=out_specs, check_vma=False
    )
```

```python
import jax
import jax.numpy as jnp
from jax import lax
from jax.experimental import pallas as pl
from jax.experimental.pallas import tpu as pltpu
from jax.sharding import PartitionSpec as P

NX, NY, NCORE, NZ = 4, 4, 2, 4
G = 4
LB, LC, LD = 1, 2, 3
MESH = pl.DeviceIdType.MESH
BF = jnp.bfloat16
F32 = jnp.float32


def kernel(
    t_hbm, w_hbm, meta_hbm, order_ref, out_hbm,
    wbuf, tm, tbuf, acc, chb, scb, mb, mc, md,
    local_sem, out_sem, send_sem, recv_sem, msend, mrecv,
):
    rows, width = t_hbm.shape
    chan = lax.axis_index("chan")
    z = lax.axis_index("int")
    core = chan % NCORE
    y = (chan // NCORE) % NY
    x = chan // (NCORE * NY)

    def at_xy(px, py, pc):
        return {"chan": (px * NY + py) * NCORE + pc}

    xs = [at_xy((x + d) % NX, y, core) for d in (1, 2, 3)]
    ys = [at_xy(x, (y + d) % NY, core) for d in (1, 2, 3)]
    zp, zm = {"int": (z + 1) % NZ}, {"int": (z + NZ - 1) % NZ}
    sib = at_xy(x, y, 1 - core)
    links = (xs[0], xs[2], ys[0], ys[2], zp, zm, sib)
    XP, XM, YP, YM, ZP, ZM, SIB = range(7)
    steps = 3 * G

    t_copy = pltpu.make_async_copy(t_hbm, tbuf, local_sem.at[G])
    t_copy.start()
    keep_core = pltpu.make_async_copy(meta_hbm.at[:, :, core], mb.at[:, :, core], msend.at[7])
    keep_core.start()

    barrier = pltpu.get_barrier_semaphore()
    peers = [sib, zp, zm] + xs + ys
    for peer in peers:
        pl.semaphore_signal(barrier, inc=1, device_id=peer, device_id_type=MESH)
    pl.semaphore_wait(barrier, len(peers))

    def spot(dq, g, c, kq):
        return ((dq * G + g) * 4 + c) * 4 + kq

    def send(link, src, dst, index):
        pltpu.make_async_remote_copy(
            src_ref=src,
            dst_ref=dst,
            send_sem=send_sem.at[link],
            recv_sem=recv_sem.at[index - G * 16],
            device_id=links[link],
            device_id_type=MESH,
        ).start()

    def forward(link, index):
        send(link, wbuf.at[index], wbuf.at[index], index)

    def arrive(index):
        pltpu.make_async_copy(wbuf.at[index], wbuf.at[index], recv_sem.at[index - G * 16]).wait()

    def tell(src, dst, slot, device):
        return pltpu.make_async_remote_copy(
            src_ref=src, dst_ref=dst, send_sem=msend.at[slot], recv_sem=mrecv.at[slot],
            device_id=device, device_id_type=MESH,
        )

    cx, cy = 2 * core, 2 * core + 1

    def send_own(g):
        for c, kq in ((cx, x), (cy, y)):
            up, down = spot(3, g, c, kq), spot(1, g, c, kq)
            send(ZP, w_hbm.at[c, kq, g], wbuf.at[up], up)
            send(ZM, w_hbm.at[c, kq, g], wbuf.at[down], down)

    send_own(0)
    tells = [tell(meta_hbm.at[:, :, 1 - core], mb.at[:, :, core], 0, sib)]
    tells[0].start()
    for g in range(1, G):
        send_own(g)
    for g in range(G):
        for c in range(4):
            pltpu.make_async_copy(w_hbm.at[c, :, g], wbuf.at[pl.ds(g * 16 + c * 4, 4)], local_sem.at[g]).start()
    keep_core.wait()
    tells[0].wait_recv()
    for d in (1, 2, 3):
        tells.append(tell(mb.at[:, (y + d) % NY], mc.at[:, y], d, ys[d - 1]))
        tells[-1].start()
    keep_y = pltpu.make_async_copy(mb.at[:, y], mc.at[:, y], msend.at[8])
    keep_y.start()
    keep_y.wait()
    for d in (1, 2, 3):
        tells[d].wait_recv()
    for d in (1, 2, 3):
        tells.append(tell(mc.at[(x + d) % NX], md.at[x], 3 + d, xs[d - 1]))
        tells[-1].start()
    keep_x = pltpu.make_async_copy(mc.at[x], md.at[x], msend.at[9])
    keep_x.start()
    keep_x.wait()
    for d in (4, 5, 6):
        tells[d].wait_recv()

    @pl.loop(0, rows // 128)
    def _(m):
        first = m * 128
        row = lax.broadcasted_iota(jnp.int32, (128, 128), 0) + first
        ids = jnp.zeros((128, 128), F32)
        scale = jnp.zeros((128, 128), F32)
        for i in range(8):
            pair = md[i // 2, (i % 2) * 2, 0] + md[i // 2, (i % 2) * 2, 1]
            pair = pair + (md[i // 2, (i % 2) * 2 + 1, 0] + md[i // 2, (i % 2) * 2 + 1, 1])
            hit = row == order_ref[i : i + 1, :]
            ids = ids + jnp.where(hit, pair[0:1, :], jnp.float32(0.0))
            scale = scale + jnp.where(hit, pair[1:2, :], jnp.float32(0.0))
        r = pl.ds(pl.multiple_of(first, 128), 128)
        chb[r, :] = jnp.broadcast_to(jnp.sum(ids, axis=1, keepdims=True), (128, 128))
        scb[r, :] = jnp.broadcast_to(jnp.sum(scale, axis=1, keepdims=True), (128, 128))

    t_copy.wait()

    def mask_rows(g):
        @pl.loop(0, rows // 128)
        def _(m):
            r = pl.ds(pl.multiple_of(m * 128, 128), 128)
            for c in range(4):
                keep = jnp.where(chb[r, :] == jnp.float32(c), jnp.float32(1.0), jnp.float32(0.0)).astype(BF)
                for kq in range(4):
                    v = tbuf[r, pl.ds(pl.multiple_of((kq * G + g) * 128, 128), 128)]
                    tm[g, r, (c * 4 + kq) * 128 : (c * 4 + kq + 1) * 128] = v * keep

    def place(s):
        early = 1 - s // (2 * G)
        dq = early * (1 + 2 * (s % 2)) + (1 - early) * 2
        g = early * (s // 2) + (1 - early) * (s - 2 * G)
        return dq, g

    def unit(dq, g, slot):
        @pl.when(g == 0)
        def _():
            acc[slot] = jnp.zeros((rows, 512), F32)

        rhs = wbuf[pl.ds((dq * G + g) * 16, 16)].reshape(2048, 512)
        acc[slot] += jnp.dot(tm[g], rhs, preferred_element_type=F32)

        @pl.when(g == G - 1)
        def _():
            first = ((z + dq) % NZ) * 512
            col = pl.ds(pl.multiple_of(first, 512), 512)

            @pl.loop(0, rows // 128)
            def _(m):
                r = pl.ds(pl.multiple_of(m * 128, 128), 128)
                for part in range(4):
                    lanes = pl.ds(pl.multiple_of(first + part * 128, 128), 128)
                    obuf[r, lanes] = (acc[slot, r, part * 128 : (part + 1) * 128] * scb[r, :]).astype(BF)

            pltpu.make_async_copy(obuf.at[:, col], out_hbm.at[:, col], out_sem.at[dq]).start()

    obuf = tbuf

    def step(s, carry):
        @pl.when(s < steps)
        def _():
            dq, g = place(s)
            for c, kq, plus, minus in ((cx, x, XP, XM), (cy, y, YP, YM)):
                index = spot(dq, g, c, kq)
                arrive(index)
                forward(plus, index)
                forward(minus, index)
                forward(SIB, index)

            @pl.when(dq == 3)
            def _():
                index = spot(2, g, cx, x)
                send(ZP, wbuf.at[spot(3, g, cx, x)], wbuf.at[index], index)

            @pl.when(dq == 1)
            def _():
                index = spot(2, g, cy, y)
                send(ZM, wbuf.at[spot(1, g, cy, y)], wbuf.at[index], index)

        @pl.when(jnp.logical_and(s >= LB, s < steps + LB))
        def _():
            dq, g = place(s - LB)
            for c, kq, plus, minus in ((cx, x, XP, XM), (cy, y, YP, YM)):
                below, above = spot(dq, g, c, (kq + 3) % 4), spot(dq, g, c, (kq + 1) % 4)
                arrive(below)
                arrive(above)
                send(plus, wbuf.at[below, 0:64], wbuf.at[below, 0:64], below)
                send(minus, wbuf.at[above, 64:128], wbuf.at[above, 64:128], above)
                forward(SIB, below)
                forward(SIB, above)

        @pl.when(s < G)
        def _():
            mask_rows(s)
            own = wbuf.at[pl.ds(s * 16, 16)]
            pltpu.make_async_copy(own, own, local_sem.at[s]).wait()
            unit(0, s, 1)

        @pl.when(s >= LD)
        def _():
            dq, g = place(s - LD)
            for c in (2 - 2 * core, 3 - 2 * core):
                for kq in range(4):
                    arrive(spot(dq, g, c, kq))
            unit(dq, g, dq - 1)

        @pl.when(jnp.logical_and(s >= LC, s < steps + LC))
        def _():
            dq, g = place(s - LC)
            for c, kq in ((cx, x), (cy, y)):
                index = spot(dq, g, c, (kq + 2) % 4)
                arrive(index)
                forward(SIB, index)

        return carry

    lax.fori_loop(0, steps + LD, step, 0)

    for link, count in ((XP, 18), (XM, 18), (YP, 18), (YM, 18), (ZP, 12), (ZM, 12), (SIB, 96)):
        whole = wbuf.at[pl.ds(0, count * G // 4)]
        pltpu.make_async_copy(whole, whole, send_sem.at[link]).wait()
    for one in tells:
        one.wait_send()
    for dq in range(4):
        part = pl.ds(0, 512)
        pltpu.make_async_copy(tbuf.at[:, part], out_hbm.at[:, part], out_sem.at[dq]).wait()


def slot_values(recv_order, ph_channel, recouple_weight, rows):
    start = lax.axis_index("int") * rows
    ids = lax.dynamic_slice(ph_channel, (start,), (rows,)).astype(F32)
    scale = lax.dynamic_slice(recouple_weight, (start,), (rows,))
    hit = recv_order[None, :] == jnp.arange(rows, dtype=jnp.int32)[:, None]
    both = [jnp.sum(jnp.where(hit, v[None, :], jnp.float32(0.0)), axis=1) for v in (ids, scale)]
    quota = rows // lax.axis_size("chan")
    lanes = jnp.stack(both).reshape(2, NX, NY, NCORE, quota).transpose(1, 2, 3, 0, 4)
    mine = (jnp.arange(128) // quota) == lax.axis_index("chan") % (128 // quota)
    return jnp.where(mine, jnp.tile(lanes, (1, 1, 1, 1, 128 // quota)), jnp.float32(0.0))


def on_device(t_pp, interaction, send_order, recv_order, ph_channel, recouple_weight):
    rows = t_pp.shape[0]
    meta = slot_values(recv_order, ph_channel, recouple_weight, rows)
    pieces = interaction.reshape(4, 4, G, 128, 512)
    anyspace = pl.BlockSpec(memory_space=pl.ANY)
    vmem = pl.BlockSpec(memory_space=pltpu.VMEM)
    meta_shape = (NX, NY, NCORE, 2, 128)
    return pl.pallas_call(
        kernel,
        out_shape=jax.ShapeDtypeStruct(t_pp.shape, BF),
        in_specs=[anyspace, anyspace, anyspace, vmem],
        out_specs=anyspace,
        scratch_shapes=[
            pltpu.VMEM((4 * G * 16, 128, 512), BF),
            pltpu.VMEM((G, rows, 2048), BF),
            pltpu.VMEM((rows, 2048), BF),
            pltpu.VMEM((3, rows, 512), F32),
            pltpu.VMEM((rows, 128), F32),
            pltpu.VMEM((rows, 128), F32),
            pltpu.VMEM(meta_shape, F32),
            pltpu.VMEM(meta_shape, F32),
            pltpu.VMEM(meta_shape, F32),
            pltpu.SemaphoreType.DMA((G + 1,)),
            pltpu.SemaphoreType.DMA((4,)),
            pltpu.SemaphoreType.DMA((7,)),
            pltpu.SemaphoreType.DMA((3 * G * 16,)),
            pltpu.SemaphoreType.DMA((10,)),
            pltpu.SemaphoreType.DMA((7,)),
        ],
        compiler_params=pltpu.CompilerParams(
            collective_id=0, has_side_effects=True, vmem_limit_bytes=66 * 1000 * 1000
        ),
    )(t_pp, pieces, meta, send_order.reshape(rows // 128, 128))


def solution(mesh):
    in_specs = (
        P(("chan", "int"), None),
        P(None, None, "int"),
        P(("chan", "int")),
        P(("chan", "int")),
        P("chan"),
        P("chan"),
    )
    out_specs = P(("chan", "int"), None)
    return jax.shard_map(
        on_device, mesh=mesh, in_specs=in_specs, out_specs=out_specs, check_vma=False
    )
```

```python
import jax
import jax.numpy as jnp
from jax import lax
from jax.experimental import pallas as pl
from jax.experimental.pallas import tpu as pltpu
from jax.sharding import PartitionSpec as P

NX, NY, NCORE, NZ = 4, 4, 2, 4
G, GK, NB = 8, 4, 256
LEAD, LC, LD, PURE, PURE_IN = 4, 3, 5, 8, 16
KINDS = 7
MESH = pl.DeviceIdType.MESH
BF = jnp.bfloat16
F32 = jnp.float32


def kernel(
    t_hbm, w_hbm, meta_hbm, order_ref, out_hbm,
    wbuf, tm, tbuf, acc, chb, scb, mb, mc, md,
    local_sem, out_sem, send_sem, recv_sem, msend, mrecv,
):
    rows, width = t_hbm.shape
    chan = lax.axis_index("chan")
    z = lax.axis_index("int")
    core = chan % NCORE
    y = (chan // NCORE) % NY
    x = chan // (NCORE * NY)

    def at_xy(px, py, pc):
        return {"chan": (px * NY + py) * NCORE + pc}

    xs = [at_xy((x + d) % NX, y, core) for d in (1, 2, 3)]
    ys = [at_xy(x, (y + d) % NY, core) for d in (1, 2, 3)]
    zp, zm = {"int": (z + 1) % NZ}, {"int": (z + NZ - 1) % NZ}
    sib = at_xy(x, y, 1 - core)
    links = (xs[0], xs[2], ys[0], ys[2], zp, zm, sib)
    XP, XM, YP, YM, ZP, ZM, SIB = range(7)
    ring = G - 1
    steps = 3 * ring
    obuf = tbuf

    t_copy = pltpu.make_async_copy(t_hbm, tbuf, local_sem.at[G])
    t_copy.start()
    keep_core = pltpu.make_async_copy(meta_hbm.at[:, :, core], mb.at[:, :, core], msend.at[7])
    keep_core.start()

    barrier = pltpu.get_barrier_semaphore()
    peers = [sib, zp, zm] + xs + ys
    for peer in peers:
        pl.semaphore_signal(barrier, inc=1, device_id=peer, device_id_type=MESH)
    pl.semaphore_wait(barrier, len(peers))

    def spot(dq, g, c, kq):
        return ((dq * G + g) * 4 + c) * 4 + kq

    def send(link, src, index, kind, rows_of=None):
        dst = wbuf.at[index] if rows_of is None else wbuf.at[index, rows_of[0] : rows_of[1]]
        pltpu.make_async_remote_copy(
            src_ref=src,
            dst_ref=dst,
            send_sem=send_sem.at[link],
            recv_sem=recv_sem.at[(index // 16 - G) * KINDS + kind],
            device_id=links[link],
            device_id_type=MESH,
        ).start()

    def forward(link, index, kind):
        send(link, wbuf.at[index], index, kind)

    def arrive(index, kind, count=1):
        whole = wbuf.at[pl.ds(index, count)]
        pltpu.make_async_copy(whole, whole, recv_sem.at[(index // 16 - G) * KINDS + kind]).wait()

    def tell(src, dst, slot, device):
        return pltpu.make_async_remote_copy(
            src_ref=src, dst_ref=dst, send_sem=msend.at[slot], recv_sem=mrecv.at[slot],
            device_id=device, device_id_type=MESH,
        )

    cx, cy = 2 * core, 2 * core + 1

    def piece(c, kq, g):
        return w_hbm.at[c, kq, g % GK, :, pl.ds((g // GK) * NB, NB)]

    def send_own(link, dq, c, kq, g, kind):
        send(link, piece(c, kq, g), spot(dq, g, c, kq), kind)

    def send_ring(g):
        send_own(ZP, 3, cx, x, g, 1)
        send_own(ZM, 1, cy, y, g, 2)
        send_own(ZP, 3, cy, y, g, 2)
        send_own(ZM, 1, cx, x, g, 1)

    send_ring(0)
    tells = [tell(meta_hbm.at[:, :, 1 - core], mb.at[:, :, core], 0, sib)]
    tells[0].start()
    for g in range(1, ring):
        send_ring(g)
    for g in range(G):
        for c in range(4):
            src = w_hbm.at[c, :, g % GK, :, pl.ds((g // GK) * NB, NB)]
            pltpu.make_async_copy(src, wbuf.at[pl.ds(g * 16 + c * 4, 4)], local_sem.at[g]).start()
    keep_core.wait()
    tells[0].wait_recv()
    for d in (1, 2, 3):
        tells.append(tell(mb.at[:, (y + d) % NY], mc.at[:, y], d, ys[d - 1]))
        tells[-1].start()
    keep_y = pltpu.make_async_copy(mb.at[:, y], mc.at[:, y], msend.at[8])
    keep_y.start()
    keep_y.wait()
    for d in (1, 2, 3):
        tells[d].wait_recv()
    for d in (1, 2, 3):
        tells.append(tell(mc.at[(x + d) % NX], md.at[x], 3 + d, xs[d - 1]))
        tells[-1].start()
    keep_x = pltpu.make_async_copy(mc.at[x], md.at[x], msend.at[9])
    keep_x.start()

    def place(s, along_y):
        early = 1 - s // (2 * ring)
        odd = (s + along_y) % 2
        dq = early * (3 - 2 * odd) + (1 - early) * 2
        g = early * (s // 2) + (1 - early) * (s - 2 * ring)
        return dq, g

    def first_arrivals(s):
        for along_y, c, kq, plus, minus in ((0, cx, x, XP, XM), (1, cy, y, YP, YM)):
            dq, g = place(s, along_y)
            index = spot(dq, g, c, kq)
            arrive(index, 1 + along_y)
            forward(plus, index, 3 + along_y)
            forward(minus, index, 3 + along_y)
            forward(SIB, index, 0)

        @pl.when(jnp.logical_and(s % 2 == 0, s < 2 * ring))
        def _():
            g = s // 2
            send(ZP, wbuf.at[spot(3, g, cx, x)], spot(2, g, cx, x), 1)
            send(ZM, wbuf.at[spot(1, g, cy, y)], spot(2, g, cy, y), 2)

    for s in range(2):
        first_arrivals(jnp.int32(s))

    keep_x.wait()
    for d in (4, 5, 6):
        tells[d].wait_recv()

    @pl.loop(0, rows // 128)
    def _(m):
        first = m * 128
        row = lax.broadcasted_iota(jnp.int32, (128, 128), 0) + first
        ids = jnp.zeros((128, 128), F32)
        scale = jnp.zeros((128, 128), F32)
        for i in range(8):
            pair = md[i // 2, (i % 2) * 2, 0] + md[i // 2, (i % 2) * 2, 1]
            pair = pair + (md[i // 2, (i % 2) * 2 + 1, 0] + md[i // 2, (i % 2) * 2 + 1, 1])
            hit = row == order_ref[i : i + 1, :]
            ids = ids + jnp.where(hit, pair[0:1, :], jnp.float32(0.0))
            scale = scale + jnp.where(hit, pair[1:2, :], jnp.float32(0.0))
        r = pl.ds(pl.multiple_of(first, 128), 128)
        chb[r, :] = jnp.broadcast_to(jnp.sum(ids, axis=1, keepdims=True), (128, 128))
        scb[r, :] = jnp.broadcast_to(jnp.sum(scale, axis=1, keepdims=True), (128, 128))

    t_copy.wait()

    def mask_rows(g):
        @pl.loop(0, rows // 128)
        def _(m):
            r = pl.ds(pl.multiple_of(m * 128, 128), 128)
            for c in range(4):
                keep = jnp.where(chb[r, :] == jnp.float32(c), jnp.float32(1.0), jnp.float32(0.0)).astype(BF)
                for kq in range(4):
                    v = tbuf[r, pl.ds(pl.multiple_of((kq * GK + g) * 128, 128), 128)]
                    tm[g, r, (c * 4 + kq) * 128 : (c * 4 + kq + 1) * 128] = v * keep

    def unit(dq, g, slot):
        gk = g % GK
        nh = g // GK
        cols = pl.ds(pl.multiple_of(nh * NB, NB), NB)

        @pl.when(gk == 0)
        def _():
            acc[slot, :, cols] = jnp.zeros((rows, NB), F32)

        rhs = wbuf[pl.ds((dq * G + g) * 16, 16)].reshape(2048, NB)
        acc[slot, :, cols] += jnp.dot(tm[gk], rhs, preferred_element_type=F32)

        @pl.when(gk == GK - 1)
        def _():
            first = ((z + dq) % NZ) * 512 + nh * NB
            col = pl.ds(pl.multiple_of(first, NB), NB)

            @pl.loop(0, rows // 128)
            def _(m):
                r = pl.ds(pl.multiple_of(m * 128, 128), 128)
                for part in range(NB // 128):
                    src = pl.ds(pl.multiple_of(nh * NB + part * 128, 128), 128)
                    dst = pl.ds(pl.multiple_of(first + part * 128, 128), 128)
                    obuf[r, dst] = (acc[slot, r, src] * scb[r, :]).astype(BF)

            pltpu.make_async_copy(obuf.at[:, col], out_hbm.at[:, col], out_sem.at[dq * 2 + nh]).start()

    def work(dq, g):
        arrive(spot(dq, g, 2 - 2 * core, 0), 0, 8)
        unit(dq, g, dq - 1)

    def step(s, carry):
        grown = jnp.minimum(s // 2, LEAD - 2)
        count = 1 + (s % 2) * (1 - jnp.minimum(s // (2 * (LEAD - 2)), 1))
        count = jnp.maximum(jnp.minimum(count, steps - (s + 2 + grown)), 0)

        def more(k, inner):
            first_arrivals(s + 2 + grown + k)
            return inner

        lax.fori_loop(0, count, more, 0)

        @pl.when(s < steps)
        def _():
            for along_y, c, kq, plus, minus in ((0, cx, x, XP, XM), (1, cy, y, YP, YM)):
                dq, g = place(s, along_y)
                below, above = spot(dq, g, c, (kq + 3) % 4), spot(dq, g, c, (kq + 1) % 4)
                arrive(spot(dq, g, c, 0), 3 + along_y, 2)
                send(plus, wbuf.at[below, 0:64], below, 5 + along_y, (0, 64))
                send(minus, wbuf.at[above, 64:128], above, 5 + along_y, (64, 128))
                forward(SIB, below, 0)
                forward(SIB, above, 0)

        @pl.when(s == PURE)
        def _():
            for kq in range(4):
                for c in (cx, cy):
                    send_own(ZP, 3, c, kq, G - 1, 1 + kq)
                    send_own(ZM, 1, c, kq, G - 1, 1 + kq)

        @pl.when(jnp.logical_and(s >= PURE_IN, s < PURE_IN + 4))
        def _():
            kq = s - PURE_IN
            for dq in (3, 1):
                arrive(spot(dq, G - 1, 0, 0), 1 + kq, 2)
            send(ZP, wbuf.at[spot(3, G - 1, cx, kq)], spot(2, G - 1, cx, kq), 1 + kq)
            send(ZM, wbuf.at[spot(1, G - 1, cy, kq)], spot(2, G - 1, cy, kq), 1 + kq)
            for dq in (3, 1):
                for c in (cx, cy):
                    forward(SIB, spot(dq, G - 1, c, kq), 0)

        @pl.when(s < G)
        def _():
            @pl.when(s < GK)
            def _():
                mask_rows(s)

            own = wbuf.at[pl.ds(s * 16, 16)]
            pltpu.make_async_copy(own, own, local_sem.at[s]).wait()
            unit(0, s, 1)

        @pl.when(s >= LD)
        def _():
            work(*place(s - LD, 0))

        @pl.when(jnp.logical_and(s >= steps, s < steps + 2))
        def _():
            work(3 - 2 * (s - steps), G - 1)

        @pl.when(jnp.logical_and(s >= LC, s < steps + LC))
        def _():
            for along_y, c, kq in ((0, cx, x), (1, cy, y)):
                dq, g = place(s - LC, along_y)
                index = spot(dq, g, c, (kq + 2) % 4)
                arrive(index, 5 + along_y)
                forward(SIB, index, 0)

        return carry

    lax.fori_loop(0, steps + LC, step, 0)

    for kq in range(4):
        arrive(spot(2, G - 1, 0, 0), 1 + kq, 2)
        for c in (cx, cy):
            forward(SIB, spot(2, G - 1, c, kq), 0)

    def rest(g, carry):
        work(2, g)
        return carry

    lax.fori_loop(ring - (LD - LC), G, rest, 0)

    for link in (XP, XM, YP, YM):
        whole = wbuf.at[pl.ds(0, steps * 3), 0:64]
        pltpu.make_async_copy(whole, whole, send_sem.at[link]).wait()
    for link, count in ((ZP, steps + 12), (ZM, steps + 12), (SIB, 3 * G * 8)):
        whole = wbuf.at[pl.ds(0, count)]
        pltpu.make_async_copy(whole, whole, send_sem.at[link]).wait()
    for one in tells:
        one.wait_send()
    for part in range(8):
        cols = pl.ds(0, NB)
        pltpu.make_async_copy(obuf.at[:, cols], out_hbm.at[:, cols], out_sem.at[part]).wait()


def slot_values(recv_order, ph_channel, recouple_weight, rows):
    start = lax.axis_index("int") * rows
    ids = lax.dynamic_slice(ph_channel, (start,), (rows,)).astype(F32)
    scale = lax.dynamic_slice(recouple_weight, (start,), (rows,))
    hit = recv_order[None, :] == jnp.arange(rows, dtype=jnp.int32)[:, None]
    both = [jnp.sum(jnp.where(hit, v[None, :], jnp.float32(0.0)), axis=1) for v in (ids, scale)]
    quota = rows // lax.axis_size("chan")
    lanes = jnp.stack(both).reshape(2, NX, NY, NCORE, quota).transpose(1, 2, 3, 0, 4)
    mine = (jnp.arange(128) // quota) == lax.axis_index("chan") % (128 // quota)
    return jnp.where(mine, jnp.tile(lanes, (1, 1, 1, 1, 128 // quota)), jnp.float32(0.0))


def on_device(t_pp, interaction, send_order, recv_order, ph_channel, recouple_weight):
    rows = t_pp.shape[0]
    meta = slot_values(recv_order, ph_channel, recouple_weight, rows)
    pieces = interaction.reshape(4, 4, GK, 128, 512)
    anyspace = pl.BlockSpec(memory_space=pl.ANY)
    vmem = pl.BlockSpec(memory_space=pltpu.VMEM)
    meta_shape = (NX, NY, NCORE, 2, 128)
    return pl.pallas_call(
        kernel,
        out_shape=jax.ShapeDtypeStruct(t_pp.shape, BF),
        in_specs=[anyspace, anyspace, anyspace, vmem],
        out_specs=anyspace,
        scratch_shapes=[
            pltpu.VMEM((4 * G * 16, 128, NB), BF),
            pltpu.VMEM((GK, rows, 2048), BF),
            pltpu.VMEM((rows, 2048), BF),
            pltpu.VMEM((3, rows, 512), F32),
            pltpu.VMEM((rows, 128), F32),
            pltpu.VMEM((rows, 128), F32),
            pltpu.VMEM(meta_shape, F32),
            pltpu.VMEM(meta_shape, F32),
            pltpu.VMEM(meta_shape, F32),
            pltpu.SemaphoreType.DMA((G + 1,)),
            pltpu.SemaphoreType.DMA((8,)),
            pltpu.SemaphoreType.DMA((7,)),
            pltpu.SemaphoreType.DMA((3 * G * KINDS,)),
            pltpu.SemaphoreType.DMA((10,)),
            pltpu.SemaphoreType.DMA((7,)),
        ],
        compiler_params=pltpu.CompilerParams(
            collective_id=0, has_side_effects=True, vmem_limit_bytes=66 * 1000 * 1000
        ),
    )(t_pp, pieces, meta, send_order.reshape(rows // 128, 128))


def solution(mesh):
    in_specs = (
        P(("chan", "int"), None),
        P(None, None, "int"),
        P(("chan", "int")),
        P(("chan", "int")),
        P("chan"),
        P("chan"),
    )
    out_specs = P(("chan", "int"), None)
    return jax.shard_map(
        on_device, mesh=mesh, in_specs=in_specs, out_specs=out_specs, check_vma=False
    )
```

```python
import jax
import jax.numpy as jnp
from jax import lax
from jax.experimental import pallas as pl
from jax.experimental.pallas import tpu as pltpu
from jax.sharding import PartitionSpec as P

NX, NY, NCORE, NZ = 4, 4, 2, 4
G, GK, NB = 8, 4, 256
LEAD, LC, LD, PURE, PURE_IN = 5, 3, 5, 8, 16
KINDS = 7
MESH = pl.DeviceIdType.MESH
BF = jnp.bfloat16
F32 = jnp.float32


def kernel(
    t_hbm, w_hbm, meta_hbm, order_ref, out_ref,
    own, wbuf, tm, acc, chb, scb, kb, mb, mc, md,
    local_sem, send_sem, recv_sem, msend, mrecv,
):
    rows, width = t_hbm.shape
    chan = lax.axis_index("chan")
    z = lax.axis_index("int")
    core = chan % NCORE
    y = (chan // NCORE) % NY
    x = chan // (NCORE * NY)

    def at_xy(px, py, pc):
        return {"chan": (px * NY + py) * NCORE + pc}

    xs = [at_xy((x + d) % NX, y, core) for d in (1, 2, 3)]
    ys = [at_xy(x, (y + d) % NY, core) for d in (1, 2, 3)]
    zp, zm = {"int": (z + 1) % NZ}, {"int": (z + NZ - 1) % NZ}
    sib = at_xy(x, y, 1 - core)
    links = (xs[0], xs[2], ys[0], ys[2], zp, zm, sib)
    XP, XM, YP, YM, ZP, ZM, SIB = range(7)
    ring = G - 1
    steps = 3 * ring

    t_copy = pltpu.make_async_copy(t_hbm, out_ref, local_sem.at[4])
    t_copy.start()
    own_copies = [pltpu.make_async_copy(w_hbm.at[c], own.at[c], local_sem.at[c]) for c in range(4)]
    own_copies[0].start()
    keep_core = pltpu.make_async_copy(meta_hbm.at[:, :, core], mb.at[:, :, core], msend.at[7])
    keep_core.start()

    barrier = pltpu.get_barrier_semaphore()
    peers = [sib, zp, zm] + xs + ys
    for peer in peers:
        pl.semaphore_signal(barrier, inc=1, device_id=peer, device_id_type=MESH)
    pl.semaphore_wait(barrier, len(peers))

    def spot(dq, g, c, kq):
        return (((dq - 1) * G + g) * 4 + c) * 4 + kq

    def send(link, src, index, kind, rows_of=None):
        dst = wbuf.at[index] if rows_of is None else wbuf.at[index, rows_of[0] : rows_of[1]]
        pltpu.make_async_remote_copy(
            src_ref=src,
            dst_ref=dst,
            send_sem=send_sem.at[link],
            recv_sem=recv_sem.at[(index // 16) * KINDS + kind],
            device_id=links[link],
            device_id_type=MESH,
        ).start()

    def forward(link, index, kind):
        send(link, wbuf.at[index], index, kind)

    def arrive(index, kind, count=1):
        whole = wbuf.at[pl.ds(index, count)]
        pltpu.make_async_copy(whole, whole, recv_sem.at[(index // 16) * KINDS + kind]).wait()

    def tell(src, dst, slot, device):
        return pltpu.make_async_remote_copy(
            src_ref=src, dst_ref=dst, send_sem=msend.at[slot], recv_sem=mrecv.at[slot],
            device_id=device, device_id_type=MESH,
        )

    cx, cy = 2 * core, 2 * core + 1

    def piece(c, kq, g):
        return w_hbm.at[c, kq, g % GK, :, pl.ds((g // GK) * NB, NB)]

    def send_own(link, dq, c, kq, g, kind):
        send(link, piece(c, kq, g), spot(dq, g, c, kq), kind)

    def send_ring(g):
        send_own(ZP, 3, cx, x, g, 1)
        send_own(ZM, 1, cy, y, g, 2)
        send_own(ZP, 3, cy, y, g, 2)
        send_own(ZM, 1, cx, x, g, 1)

    send_ring(0)
    tells = [tell(meta_hbm.at[:, :, 1 - core], mb.at[:, :, core], 0, sib)]
    tells[0].start()
    for g in range(1, ring):
        send_ring(g)
    for c in (1, 2, 3):
        own_copies[c].start()
    keep_core.wait()
    tells[0].wait_recv()
    for d in (1, 2, 3):
        tells.append(tell(mb.at[:, (y + d) % NY], mc.at[:, y], d, ys[d - 1]))
        tells[-1].start()
    keep_y = pltpu.make_async_copy(mb.at[:, y], mc.at[:, y], msend.at[8])
    keep_y.start()

    def place(s, along_y):
        early = 1 - s // (2 * ring)
        odd = (s + along_y) % 2
        dq = early * (3 - 2 * odd) + (1 - early) * 2
        g = early * (s // 2) + (1 - early) * (s - 2 * ring)
        return dq, g

    def first_arrivals(s):
        for along_y, c, kq, plus, minus in ((0, cx, x, XP, XM), (1, cy, y, YP, YM)):
            dq, g = place(s, along_y)
            index = spot(dq, g, c, kq)
            arrive(index, 1 + along_y)
            forward(plus, index, 3 + along_y)
            forward(minus, index, 3 + along_y)
            forward(SIB, index, 0)

        @pl.when(jnp.logical_and(s % 2 == 0, s < 2 * ring))
        def _():
            g = s // 2
            send(ZP, wbuf.at[spot(3, g, cx, x)], spot(2, g, cx, x), 1)
            send(ZM, wbuf.at[spot(1, g, cy, y)], spot(2, g, cy, y), 2)

    def raw(c):
        return jnp.dot(out_ref[...], own[c].reshape(2048, 512), preferred_element_type=F32)

    t_copy.wait()
    own_copies[0].wait()
    acc[0] = raw(0)
    keep_y.wait()
    for d in (1, 2, 3):
        tells[d].wait_recv()
    for d in (1, 2, 3):
        tells.append(tell(mc.at[(x + d) % NX], md.at[x], 3 + d, xs[d - 1]))
        tells[-1].start()
    keep_x = pltpu.make_async_copy(mc.at[x], md.at[x], msend.at[9])
    keep_x.start()
    for s in (0, 1):
        first_arrivals(jnp.int32(s))
    own_copies[1].wait()
    acc[1] = raw(1)
    for s in (2, 3):
        first_arrivals(jnp.int32(s))
    keep_x.wait()
    for d in (4, 5, 6):
        tells[d].wait_recv()

    @pl.loop(0, rows // 128)
    def _(m):
        first = m * 128
        row = lax.broadcasted_iota(jnp.int32, (128, 128), 0) + first
        ids = jnp.zeros((128, 128), F32)
        scale = jnp.zeros((128, 128), F32)
        for i in range(8):
            pair = md[i // 2, (i % 2) * 2, 0] + md[i // 2, (i % 2) * 2, 1]
            pair = pair + (md[i // 2, (i % 2) * 2 + 1, 0] + md[i // 2, (i % 2) * 2 + 1, 1])
            hit = row == order_ref[i : i + 1, :]
            ids = ids + jnp.where(hit, pair[0:1, :], jnp.float32(0.0))
            scale = scale + jnp.where(hit, pair[1:2, :], jnp.float32(0.0))
        r = pl.ds(pl.multiple_of(first, 128), 128)
        ids = jnp.broadcast_to(jnp.sum(ids, axis=1, keepdims=True), (128, 128))
        chb[r, :] = ids
        for c in range(4):
            kb[c, r, :] = jnp.where(ids == jnp.float32(c), jnp.float32(1.0), jnp.float32(0.0)).astype(BF)
        scb[r, :] = jnp.broadcast_to(jnp.sum(scale, axis=1, keepdims=True), (128, 128))

    own_copies[2].wait()
    acc[2] = raw(2)
    first_arrivals(jnp.int32(4))

    def mask_rows(g):
        @pl.loop(0, rows // 128)
        def _(m):
            r = pl.ds(pl.multiple_of(m * 128, 128), 128)
            for c in range(4):
                for kq in range(4):
                    v = out_ref[r, pl.ds(pl.multiple_of((kq * GK + g) * 128, 128), 128)]
                    tm[g, r, (c * 4 + kq) * 128 : (c * 4 + kq + 1) * 128] = v * kb[c, r, :]

    def finish_own():
        own_copies[3].wait()
        wide = raw(3)
        for m in range(rows // 128):
            r = slice(m * 128, (m + 1) * 128)
            ids, scale = chb[r, :], scb[r, :]
            for part in range(4):
                col = slice(part * 128, (part + 1) * 128)
                v = jnp.where(ids == jnp.float32(3), wide[r, col], jnp.float32(0.0))
                for c in range(3):
                    v = jnp.where(ids == jnp.float32(c), acc[c, r, col], v)
                out_ref[r, pl.ds(pl.multiple_of(z * 512 + part * 128, 128), 128)] = (v * scale).astype(BF)

    def unit(dq, g, slot):
        gk = g % GK
        nh = g // GK
        cols = pl.ds(pl.multiple_of(nh * NB, NB), NB)

        @pl.when(gk == 0)
        def _():
            acc[slot, :, cols] = jnp.zeros((rows, NB), F32)

        rhs = wbuf[pl.ds(((dq - 1) * G + g) * 16, 16)].reshape(2048, NB)
        acc[slot, :, cols] += jnp.dot(tm[gk], rhs, preferred_element_type=F32)

        @pl.when(gk == GK - 1)
        def _():
            first = ((z + dq) % NZ) * 512 + nh * NB

            @pl.loop(0, rows // 128)
            def _(m):
                r = pl.ds(pl.multiple_of(m * 128, 128), 128)
                for part in range(NB // 128):
                    src = pl.ds(pl.multiple_of(nh * NB + part * 128, 128), 128)
                    dst = pl.ds(pl.multiple_of(first + part * 128, 128), 128)
                    out_ref[r, dst] = (acc[slot, r, src] * scb[r, :]).astype(BF)


    def work(dq, g):
        arrive(spot(dq, g, 2 - 2 * core, 0), 0, 8)
        unit(dq, g, dq - 1)

    def step(s, carry):
        @pl.when(s + LEAD < steps)
        def _():
            first_arrivals(s + LEAD)

        @pl.when(s < steps)
        def _():
            for along_y, c, kq, plus, minus in ((0, cx, x, XP, XM), (1, cy, y, YP, YM)):
                dq, g = place(s, along_y)
                below, above = spot(dq, g, c, (kq + 3) % 4), spot(dq, g, c, (kq + 1) % 4)
                arrive(spot(dq, g, c, 0), 3 + along_y, 2)
                send(plus, wbuf.at[below, 0:64], below, 5 + along_y, (0, 64))
                send(minus, wbuf.at[above, 64:128], above, 5 + along_y, (64, 128))
                forward(SIB, below, 0)
                forward(SIB, above, 0)

        @pl.when(s == PURE)
        def _():
            for kq in range(4):
                for c in (cx, cy):
                    send_own(ZP, 3, c, kq, G - 1, 1 + kq)
                    send_own(ZM, 1, c, kq, G - 1, 1 + kq)

        @pl.when(jnp.logical_and(s >= PURE_IN, s < PURE_IN + 4))
        def _():
            kq = s - PURE_IN
            for dq in (3, 1):
                arrive(spot(dq, G - 1, 0, 0), 1 + kq, 2)
            send(ZP, wbuf.at[spot(3, G - 1, cx, kq)], spot(2, G - 1, cx, kq), 1 + kq)
            send(ZM, wbuf.at[spot(1, G - 1, cy, kq)], spot(2, G - 1, cy, kq), 1 + kq)
            for dq in (3, 1):
                for c in (cx, cy):
                    forward(SIB, spot(dq, G - 1, c, kq), 0)

        @pl.when(s < GK)
        def _():
            mask_rows(s)

        @pl.when(s == GK)
        def _():
            finish_own()

        @pl.when(s >= LD)
        def _():
            work(*place(s - LD, 0))

        @pl.when(jnp.logical_and(s >= steps, s < steps + 2))
        def _():
            work(3 - 2 * (s - steps), G - 1)

        @pl.when(jnp.logical_and(s >= LC, s < steps + LC))
        def _():
            for along_y, c, kq in ((0, cx, x), (1, cy, y)):
                dq, g = place(s - LC, along_y)
                index = spot(dq, g, c, (kq + 2) % 4)
                arrive(index, 5 + along_y)
                forward(SIB, index, 0)

        return carry

    lax.fori_loop(0, steps + LC, step, 0)

    for kq in range(4):
        arrive(spot(2, G - 1, 0, 0), 1 + kq, 2)
        for c in (cx, cy):
            forward(SIB, spot(2, G - 1, c, kq), 0)

    def rest(g, carry):
        work(2, g)
        return carry

    lax.fori_loop(ring - (LD - LC), G, rest, 0)

    for link in (XP, XM, YP, YM):
        whole = wbuf.at[pl.ds(0, steps * 3), 0:64]
        pltpu.make_async_copy(whole, whole, send_sem.at[link]).wait()
    for link, count in ((ZP, steps + 12), (ZM, steps + 12), (SIB, 3 * G * 8)):
        whole = wbuf.at[pl.ds(0, count)]
        pltpu.make_async_copy(whole, whole, send_sem.at[link]).wait()
    for one in tells:
        one.wait_send()


def slot_values(recv_order, ph_channel, recouple_weight, rows):
    start = lax.axis_index("int") * rows
    ids = lax.dynamic_slice(ph_channel, (start,), (rows,)).astype(F32)
    scale = lax.dynamic_slice(recouple_weight, (start,), (rows,))
    hit = recv_order[None, :] == jnp.arange(rows, dtype=jnp.int32)[:, None]
    both = [jnp.sum(jnp.where(hit, v[None, :], jnp.float32(0.0)), axis=1) for v in (ids, scale)]
    quota = rows // lax.axis_size("chan")
    lanes = jnp.stack(both).reshape(2, NX, NY, NCORE, quota).transpose(1, 2, 3, 0, 4)
    mine = (jnp.arange(128) // quota) == lax.axis_index("chan") % (128 // quota)
    return jnp.where(mine, jnp.tile(lanes, (1, 1, 1, 1, 128 // quota)), jnp.float32(0.0))


def on_device(t_pp, interaction, send_order, recv_order, ph_channel, recouple_weight):
    rows = t_pp.shape[0]
    meta = slot_values(recv_order, ph_channel, recouple_weight, rows)
    pieces = interaction.reshape(4, 4, GK, 128, 512)
    anyspace = pl.BlockSpec(memory_space=pl.ANY)
    vmem = pl.BlockSpec(memory_space=pltpu.VMEM)
    meta_shape = (NX, NY, NCORE, 2, 128)
    return pl.pallas_call(
        kernel,
        out_shape=pltpu.VMEM(t_pp.shape, BF),
        in_specs=[anyspace, anyspace, anyspace, vmem],
        out_specs=vmem,
        scratch_shapes=[
            pltpu.VMEM((4, 4, GK, 128, 512), BF),
            pltpu.VMEM((3 * G * 16, 128, NB), BF),
            pltpu.VMEM((GK, rows, 2048), BF),
            pltpu.VMEM((3, rows, 512), F32),
            pltpu.VMEM((rows, 128), F32),
            pltpu.VMEM((rows, 128), F32),
            pltpu.VMEM((4, rows, 128), BF),
            pltpu.VMEM(meta_shape, F32),
            pltpu.VMEM(meta_shape, F32),
            pltpu.VMEM(meta_shape, F32),
            pltpu.SemaphoreType.DMA((5,)),
            pltpu.SemaphoreType.DMA((7,)),
            pltpu.SemaphoreType.DMA((3 * G * KINDS,)),
            pltpu.SemaphoreType.DMA((10,)),
            pltpu.SemaphoreType.DMA((7,)),
        ],
        compiler_params=pltpu.CompilerParams(
            collective_id=0, has_side_effects=True, vmem_limit_bytes=62500000
        ),
    )(t_pp, pieces, meta, send_order.reshape(rows // 128, 128))


def solution(mesh):
    in_specs = (
        P(("chan", "int"), None),
        P(None, None, "int"),
        P(("chan", "int")),
        P(("chan", "int")),
        P("chan"),
        P("chan"),
    )
    out_specs = P(("chan", "int"), None)
    return jax.shard_map(
        on_device, mesh=mesh, in_specs=in_specs, out_specs=out_specs, check_vma=False
    )
```

```python
import jax
import jax.numpy as jnp
from jax import lax
from jax.experimental import pallas as pl
from jax.experimental.pallas import tpu as pltpu
from jax.sharding import PartitionSpec as P

NX, NY, NCORE, NZ = 4, 4, 2, 4
G, GK, NB = 8, 4, 256
LEAD, LC, LD, PURE, PURE_IN = 4, 2, 5, 5, 13
KINDS = 7
MESH = pl.DeviceIdType.MESH
BF = jnp.bfloat16
F32 = jnp.float32


def kernel(
    t_hbm, w_hbm, meta_hbm, order_ref, out_ref,
    own, wbuf, tm, acc, chb, scb, kb, mb, mc, md,
    local_sem, send_sem, recv_sem, msend, mrecv,
):
    rows, width = t_hbm.shape
    chan = lax.axis_index("chan")
    z = lax.axis_index("int")
    core = chan % NCORE
    y = (chan // NCORE) % NY
    x = chan // (NCORE * NY)

    def at_xy(px, py, pc):
        return {"chan": (px * NY + py) * NCORE + pc}

    xs = [at_xy((x + d) % NX, y, core) for d in (1, 2, 3)]
    ys = [at_xy(x, (y + d) % NY, core) for d in (1, 2, 3)]
    zp, zm = {"int": (z + 1) % NZ}, {"int": (z + NZ - 1) % NZ}
    sib = at_xy(x, y, 1 - core)
    links = (xs[0], xs[2], ys[0], ys[2], zp, zm, sib)
    XP, XM, YP, YM, ZP, ZM, SIB = range(7)
    ring = G - 1
    steps = 3 * ring

    t_copy = pltpu.make_async_copy(t_hbm, out_ref, local_sem.at[4])
    t_copy.start()
    own_copies = [pltpu.make_async_copy(w_hbm.at[c], own.at[c], local_sem.at[c]) for c in range(4)]
    own_copies[0].start()
    keep_core = pltpu.make_async_copy(meta_hbm.at[:, :, core], mb.at[:, :, core], msend.at[7])
    keep_core.start()

    barrier = pltpu.get_barrier_semaphore()
    peers = [sib, zp, zm] + xs + ys
    for peer in peers:
        pl.semaphore_signal(barrier, inc=1, device_id=peer, device_id_type=MESH)
    pl.semaphore_wait(barrier, len(peers))

    def spot(dq, g, c, kq):
        return (((dq - 1) * G + g) * 4 + c) * 4 + kq

    def send(link, src, index, kind, rows_of=None):
        dst = wbuf.at[index] if rows_of is None else wbuf.at[index, rows_of[0] : rows_of[1]]
        pltpu.make_async_remote_copy(
            src_ref=src,
            dst_ref=dst,
            send_sem=send_sem.at[link],
            recv_sem=recv_sem.at[(index // 16) * KINDS + kind],
            device_id=links[link],
            device_id_type=MESH,
        ).start()

    def forward(link, index, kind):
        send(link, wbuf.at[index], index, kind)

    def arrive(index, kind, count=1):
        whole = wbuf.at[pl.ds(index, count)]
        pltpu.make_async_copy(whole, whole, recv_sem.at[(index // 16) * KINDS + kind]).wait()

    def tell(src, dst, slot, device):
        return pltpu.make_async_remote_copy(
            src_ref=src, dst_ref=dst, send_sem=msend.at[slot], recv_sem=mrecv.at[slot],
            device_id=device, device_id_type=MESH,
        )

    cx, cy = 2 * core, 2 * core + 1

    def piece(c, kq, g):
        return w_hbm.at[c, kq, g % GK, :, pl.ds((g // GK) * NB, NB)]

    def send_own(link, dq, c, kq, g, kind):
        send(link, piece(c, kq, g), spot(dq, g, c, kq), kind)

    def send_ring(g):
        send_own(ZP, 3, cx, x, g, 1)
        send_own(ZM, 1, cy, y, g, 2)
        send_own(ZP, 3, cy, y, g, 2)
        send_own(ZM, 1, cx, x, g, 1)

    send_ring(0)
    tells = [tell(meta_hbm.at[:, :, 1 - core], mb.at[:, :, core], 0, sib)]
    tells[0].start()
    for g in range(1, ring):
        send_ring(g)
    for c in (1, 2, 3):
        own_copies[c].start()
    keep_core.wait()
    tells[0].wait_recv()
    for d in (1, 2, 3):
        tells.append(tell(mb.at[:, (y + d) % NY], mc.at[:, y], d, ys[d - 1]))
        tells[-1].start()
    keep_y = pltpu.make_async_copy(mb.at[:, y], mc.at[:, y], msend.at[8])
    keep_y.start()

    def place(s, along_y):
        early = 1 - s // (2 * ring)
        odd = (s + along_y) % 2
        dq = early * (3 - 2 * odd) + (1 - early) * 2
        g = early * (s // 2) + (1 - early) * (s - 2 * ring)
        return dq, g

    def first_arrivals(s):
        for along_y, c, kq, plus, minus in ((0, cx, x, XP, XM), (1, cy, y, YP, YM)):
            dq, g = place(s, along_y)
            index = spot(dq, g, c, kq)
            arrive(index, 1 + along_y)
            forward(plus, index, 3 + along_y)
            forward(minus, index, 3 + along_y)
            forward(SIB, index, 0)

        @pl.when(jnp.logical_and(s % 2 == 0, s < 2 * ring))
        def _():
            g = s // 2
            send(ZP, wbuf.at[spot(3, g, cx, x)], spot(2, g, cx, x), 1)
            send(ZM, wbuf.at[spot(1, g, cy, y)], spot(2, g, cy, y), 2)

    def raw(c):
        return jnp.dot(out_ref[...], own[c].reshape(2048, 512), preferred_element_type=F32)

    t_copy.wait()
    own_copies[0].wait()
    acc[0] = raw(0)
    keep_y.wait()
    for d in (1, 2, 3):
        tells[d].wait_recv()
    for d in (1, 2, 3):
        tells.append(tell(mc.at[(x + d) % NX], md.at[x], 3 + d, xs[d - 1]))
        tells[-1].start()
    keep_x = pltpu.make_async_copy(mc.at[x], md.at[x], msend.at[9])
    keep_x.start()
    for s in (0, 1):
        first_arrivals(jnp.int32(s))
    own_copies[1].wait()
    acc[1] = raw(1)
    for s in (2, 3):
        first_arrivals(jnp.int32(s))
    keep_x.wait()
    for d in (4, 5, 6):
        tells[d].wait_recv()

    @pl.loop(0, rows // 128)
    def _(m):
        first = m * 128
        row = lax.broadcasted_iota(jnp.int32, (128, 128), 0) + first
        ids = jnp.zeros((128, 128), F32)
        scale = jnp.zeros((128, 128), F32)
        for i in range(8):
            pair = md[i // 2, (i % 2) * 2, 0] + md[i // 2, (i % 2) * 2, 1]
            pair = pair + (md[i // 2, (i % 2) * 2 + 1, 0] + md[i // 2, (i % 2) * 2 + 1, 1])
            hit = row == order_ref[i : i + 1, :]
            ids = ids + jnp.where(hit, pair[0:1, :], jnp.float32(0.0))
            scale = scale + jnp.where(hit, pair[1:2, :], jnp.float32(0.0))
        r = pl.ds(pl.multiple_of(first, 128), 128)
        ids = jnp.broadcast_to(jnp.sum(ids, axis=1, keepdims=True), (128, 128))
        chb[r, :] = ids
        for c in range(4):
            kb[c, r, :] = jnp.where(ids == jnp.float32(c), jnp.float32(1.0), jnp.float32(0.0)).astype(BF)
        scb[r, :] = jnp.broadcast_to(jnp.sum(scale, axis=1, keepdims=True), (128, 128))

    own_copies[2].wait()
    acc[2] = raw(2)

    def mask_rows(g):
        @pl.loop(0, rows // 128)
        def _(m):
            r = pl.ds(pl.multiple_of(m * 128, 128), 128)
            for c in range(4):
                for kq in range(4):
                    v = out_ref[r, pl.ds(pl.multiple_of((kq * GK + g) * 128, 128), 128)]
                    tm[g, r, (c * 4 + kq) * 128 : (c * 4 + kq + 1) * 128] = v * kb[c, r, :]

    def finish_own():
        own_copies[3].wait()
        wide = raw(3)
        for m in range(rows // 128):
            r = slice(m * 128, (m + 1) * 128)
            ids, scale = chb[r, :], scb[r, :]
            for part in range(4):
                col = slice(part * 128, (part + 1) * 128)
                v = jnp.where(ids == jnp.float32(3), wide[r, col], jnp.float32(0.0))
                for c in range(3):
                    v = jnp.where(ids == jnp.float32(c), acc[c, r, col], v)
                out_ref[r, pl.ds(pl.multiple_of(z * 512 + part * 128, 128), 128)] = (v * scale).astype(BF)

    def unit(dq, g, slot):
        gk = g % GK
        nh = g // GK
        cols = pl.ds(pl.multiple_of(nh * NB, NB), NB)

        @pl.when(gk == 0)
        def _():
            acc[slot, :, cols] = jnp.zeros((rows, NB), F32)

        rhs = wbuf[pl.ds(((dq - 1) * G + g) * 16, 16)].reshape(2048, NB)
        acc[slot, :, cols] += jnp.dot(tm[gk], rhs, preferred_element_type=F32)

        @pl.when(gk == GK - 1)
        def _():
            first = ((z + dq) % NZ) * 512 + nh * NB

            @pl.loop(0, rows // 128)
            def _(m):
                r = pl.ds(pl.multiple_of(m * 128, 128), 128)
                for part in range(NB // 128):
                    src = pl.ds(pl.multiple_of(nh * NB + part * 128, 128), 128)
                    dst = pl.ds(pl.multiple_of(first + part * 128, 128), 128)
                    out_ref[r, dst] = (acc[slot, r, src] * scb[r, :]).astype(BF)


    def work(dq, g):
        arrive(spot(dq, g, 2 - 2 * core, 0), 0, 8)
        unit(dq, g, dq - 1)

    def step(s, carry):
        @pl.when(s + LEAD < steps)
        def _():
            first_arrivals(s + LEAD)

        @pl.when(s < steps)
        def _():
            for along_y, c, kq, plus, minus in ((0, cx, x, XP, XM), (1, cy, y, YP, YM)):
                dq, g = place(s, along_y)
                below, above = spot(dq, g, c, (kq + 3) % 4), spot(dq, g, c, (kq + 1) % 4)
                arrive(spot(dq, g, c, 0), 3 + along_y, 2)
                send(plus, wbuf.at[below, 0:64], below, 5 + along_y, (0, 64))
                send(minus, wbuf.at[above, 64:128], above, 5 + along_y, (64, 128))
                forward(SIB, below, 0)
                forward(SIB, above, 0)

        @pl.when(s == PURE)
        def _():
            for kq in range(4):
                for c in (cx, cy):
                    send_own(ZP, 3, c, kq, G - 1, 1 + kq)
                    send_own(ZM, 1, c, kq, G - 1, 1 + kq)

        @pl.when(jnp.logical_and(s >= PURE_IN, s < PURE_IN + 4))
        def _():
            kq = s - PURE_IN
            for dq in (3, 1):
                arrive(spot(dq, G - 1, 0, 0), 1 + kq, 2)
            send(ZP, wbuf.at[spot(3, G - 1, cx, kq)], spot(2, G - 1, cx, kq), 1 + kq)
            send(ZM, wbuf.at[spot(1, G - 1, cy, kq)], spot(2, G - 1, cy, kq), 1 + kq)
            for dq in (3, 1):
                for c in (cx, cy):
                    forward(SIB, spot(dq, G - 1, c, kq), 0)

        @pl.when(s < GK)
        def _():
            mask_rows(s)

        @pl.when(s == GK)
        def _():
            finish_own()

        @pl.when(s >= LD)
        def _():
            work(*place(s - LD, 0))

        @pl.when(jnp.logical_and(s >= steps, s < steps + 2))
        def _():
            work(3 - 2 * (s - steps), G - 1)

        @pl.when(jnp.logical_and(s >= LC, s < steps + LC))
        def _():
            for along_y, c, kq in ((0, cx, x), (1, cy, y)):
                dq, g = place(s - LC, along_y)
                index = spot(dq, g, c, (kq + 2) % 4)
                arrive(index, 5 + along_y)
                forward(SIB, index, 0)

        return carry

    lax.fori_loop(0, steps + LC, step, 0)

    for kq in range(4):
        arrive(spot(2, G - 1, 0, 0), 1 + kq, 2)
        for c in (cx, cy):
            forward(SIB, spot(2, G - 1, c, kq), 0)

    def rest(g, carry):
        work(2, g)
        return carry

    lax.fori_loop(ring - (LD - LC), G, rest, 0)

    for link in (XP, XM, YP, YM):
        whole = wbuf.at[pl.ds(0, steps * 3), 0:64]
        pltpu.make_async_copy(whole, whole, send_sem.at[link]).wait()
    for link, count in ((ZP, steps + 12), (ZM, steps + 12), (SIB, 3 * G * 8)):
        whole = wbuf.at[pl.ds(0, count)]
        pltpu.make_async_copy(whole, whole, send_sem.at[link]).wait()
    for one in tells:
        one.wait_send()


def slot_values(recv_order, ph_channel, recouple_weight, rows):
    start = lax.axis_index("int") * rows
    ids = lax.dynamic_slice(ph_channel, (start,), (rows,)).astype(F32)
    scale = lax.dynamic_slice(recouple_weight, (start,), (rows,))
    hit = recv_order[None, :] == jnp.arange(rows, dtype=jnp.int32)[:, None]
    both = [jnp.sum(jnp.where(hit, v[None, :], jnp.float32(0.0)), axis=1) for v in (ids, scale)]
    quota = rows // lax.axis_size("chan")
    lanes = jnp.stack(both).reshape(2, NX, NY, NCORE, quota).transpose(1, 2, 3, 0, 4)
    mine = (jnp.arange(128) // quota) == lax.axis_index("chan") % (128 // quota)
    return jnp.where(mine, jnp.tile(lanes, (1, 1, 1, 1, 128 // quota)), jnp.float32(0.0))


def on_device(t_pp, interaction, send_order, recv_order, ph_channel, recouple_weight):
    rows = t_pp.shape[0]
    meta = slot_values(recv_order, ph_channel, recouple_weight, rows)
    pieces = interaction.reshape(4, 4, GK, 128, 512)
    anyspace = pl.BlockSpec(memory_space=pl.ANY)
    vmem = pl.BlockSpec(memory_space=pltpu.VMEM)
    meta_shape = (NX, NY, NCORE, 2, 128)
    return pl.pallas_call(
        kernel,
        out_shape=pltpu.VMEM(t_pp.shape, BF),
        in_specs=[anyspace, anyspace, anyspace, vmem],
        out_specs=vmem,
        scratch_shapes=[
            pltpu.VMEM((4, 4, GK, 128, 512), BF),
            pltpu.VMEM((3 * G * 16, 128, NB), BF),
            pltpu.VMEM((GK, rows, 2048), BF),
            pltpu.VMEM((3, rows, 512), F32),
            pltpu.VMEM((rows, 128), F32),
            pltpu.VMEM((rows, 128), F32),
            pltpu.VMEM((4, rows, 128), BF),
            pltpu.VMEM(meta_shape, F32),
            pltpu.VMEM(meta_shape, F32),
            pltpu.VMEM(meta_shape, F32),
            pltpu.SemaphoreType.DMA((5,)),
            pltpu.SemaphoreType.DMA((7,)),
            pltpu.SemaphoreType.DMA((3 * G * KINDS,)),
            pltpu.SemaphoreType.DMA((10,)),
            pltpu.SemaphoreType.DMA((7,)),
        ],
        compiler_params=pltpu.CompilerParams(
            collective_id=0, has_side_effects=True, vmem_limit_bytes=62500000
        ),
    )(t_pp, pieces, meta, send_order.reshape(rows // 128, 128))


def solution(mesh):
    in_specs = (
        P(("chan", "int"), None),
        P(None, None, "int"),
        P(("chan", "int")),
        P(("chan", "int")),
        P("chan"),
        P("chan"),
    )
    out_specs = P(("chan", "int"), None)
    return jax.shard_map(
        on_device, mesh=mesh, in_specs=in_specs, out_specs=out_specs, check_vma=False
    )
```

```python
import jax
import jax.numpy as jnp
from jax import lax
from jax.experimental import pallas as pl
from jax.experimental.pallas import tpu as pltpu
from jax.sharding import PartitionSpec as P

NX, NY, NCORE, NZ = 4, 4, 2, 4
G, GK, NB = 8, 4, 256
LEAD, LC, LD, PURE, PURE_IN = 4, 2, 5, 4, 12
KINDS = 7
MESH = pl.DeviceIdType.MESH
BF = jnp.bfloat16
F32 = jnp.float32


def kernel(
    t_hbm, w_hbm, meta_hbm, order_ref, out_ref,
    own, wbuf, tm, acc, chb, scb, kb, mb, mc, md,
    local_sem, send_sem, recv_sem, msend, mrecv,
):
    rows, width = t_hbm.shape
    chan = lax.axis_index("chan")
    z = lax.axis_index("int")
    core = chan % NCORE
    y = (chan // NCORE) % NY
    x = chan // (NCORE * NY)

    def at_xy(px, py, pc):
        return {"chan": (px * NY + py) * NCORE + pc}

    xs = [at_xy((x + d) % NX, y, core) for d in (1, 2, 3)]
    ys = [at_xy(x, (y + d) % NY, core) for d in (1, 2, 3)]
    zp, zm = {"int": (z + 1) % NZ}, {"int": (z + NZ - 1) % NZ}
    sib = at_xy(x, y, 1 - core)
    links = (xs[0], xs[2], ys[0], ys[2], zp, zm, sib)
    XP, XM, YP, YM, ZP, ZM, SIB = range(7)
    ring = G - 1
    steps = 3 * ring

    t_copy = pltpu.make_async_copy(t_hbm, out_ref, local_sem.at[4])
    t_copy.start()
    own_copies = [pltpu.make_async_copy(w_hbm.at[c], own.at[c], local_sem.at[c]) for c in range(4)]
    own_copies[0].start()
    keep_core = pltpu.make_async_copy(meta_hbm.at[:, :, core], mb.at[:, :, core], msend.at[7])
    keep_core.start()

    barrier = pltpu.get_barrier_semaphore()
    peers = [sib, zp, zm] + xs + ys
    for peer in peers:
        pl.semaphore_signal(barrier, inc=1, device_id=peer, device_id_type=MESH)
    pl.semaphore_wait(barrier, len(peers))

    def spot(dq, g, c, kq):
        return (((dq - 1) * G + g) * 4 + c) * 4 + kq

    def send(link, src, index, kind, rows_of=None):
        dst = wbuf.at[index] if rows_of is None else wbuf.at[index, rows_of[0] : rows_of[1]]
        pltpu.make_async_remote_copy(
            src_ref=src,
            dst_ref=dst,
            send_sem=send_sem.at[link],
            recv_sem=recv_sem.at[(index // 16) * KINDS + kind],
            device_id=links[link],
            device_id_type=MESH,
        ).start()

    def forward(link, index, kind):
        send(link, wbuf.at[index], index, kind)

    def arrive(index, kind, count=1):
        whole = wbuf.at[pl.ds(index, count)]
        pltpu.make_async_copy(whole, whole, recv_sem.at[(index // 16) * KINDS + kind]).wait()

    def tell(src, dst, slot, device):
        return pltpu.make_async_remote_copy(
            src_ref=src, dst_ref=dst, send_sem=msend.at[slot], recv_sem=mrecv.at[slot],
            device_id=device, device_id_type=MESH,
        )

    cx, cy = 2 * core, 2 * core + 1

    def piece(c, kq, g):
        return w_hbm.at[c, kq, g % GK, :, pl.ds((g // GK) * NB, NB)]

    def send_own(link, dq, c, kq, g, kind):
        send(link, piece(c, kq, g), spot(dq, g, c, kq), kind)

    def send_ring(g):
        send_own(ZP, 3, cx, x, g, 1)
        send_own(ZM, 1, cy, y, g, 2)
        send_own(ZP, 3, cy, y, g, 2)
        send_own(ZM, 1, cx, x, g, 1)

    send_ring(0)
    tells = [tell(meta_hbm.at[:, :, 1 - core], mb.at[:, :, core], 0, sib)]
    tells[0].start()
    for g in range(1, ring):
        send_ring(g)
    for c in (1, 2, 3):
        own_copies[c].start()
    keep_core.wait()
    tells[0].wait_recv()
    for d in (1, 2, 3):
        tells.append(tell(mb.at[:, (y + d) % NY], mc.at[:, y], d, ys[d - 1]))
        tells[-1].start()
    keep_y = pltpu.make_async_copy(mb.at[:, y], mc.at[:, y], msend.at[8])
    keep_y.start()

    def place(s, along_y):
        early = 1 - s // (2 * ring)
        odd = (s + along_y) % 2
        dq = early * (3 - 2 * odd) + (1 - early) * 2
        g = early * (s // 2) + (1 - early) * (s - 2 * ring)
        return dq, g

    def first_arrivals(s):
        for along_y, c, kq, plus, minus in ((0, cx, x, XP, XM), (1, cy, y, YP, YM)):
            dq, g = place(s, along_y)
            index = spot(dq, g, c, kq)
            arrive(index, 1 + along_y)
            forward(plus, index, 3 + along_y)
            forward(minus, index, 3 + along_y)
            forward(SIB, index, 0)

        @pl.when(jnp.logical_and(s % 2 == 0, s < 2 * ring))
        def _():
            g = s // 2
            send(ZP, wbuf.at[spot(3, g, cx, x)], spot(2, g, cx, x), 1)
            send(ZM, wbuf.at[spot(1, g, cy, y)], spot(2, g, cy, y), 2)

    def raw(c):
        return jnp.dot(out_ref[...], own[c].reshape(2048, 512), preferred_element_type=F32)

    t_copy.wait()
    own_copies[0].wait()
    acc[0] = raw(0)
    keep_y.wait()
    for d in (1, 2, 3):
        tells[d].wait_recv()
    for d in (1, 2, 3):
        tells.append(tell(mc.at[(x + d) % NX], md.at[x], 3 + d, xs[d - 1]))
        tells[-1].start()
    keep_x = pltpu.make_async_copy(mc.at[x], md.at[x], msend.at[9])
    keep_x.start()
    for s in (0, 1):
        first_arrivals(jnp.int32(s))
    own_copies[1].wait()
    acc[1] = raw(1)
    for s in (2, 3):
        first_arrivals(jnp.int32(s))
    keep_x.wait()
    for d in (4, 5, 6):
        tells[d].wait_recv()

    @pl.loop(0, rows // 128)
    def _(m):
        first = m * 128
        row = lax.broadcasted_iota(jnp.int32, (128, 128), 0) + first
        ids = jnp.zeros((128, 128), F32)
        scale = jnp.zeros((128, 128), F32)
        for i in range(8):
            pair = md[i // 2, (i % 2) * 2, 0] + md[i // 2, (i % 2) * 2, 1]
            pair = pair + (md[i // 2, (i % 2) * 2 + 1, 0] + md[i // 2, (i % 2) * 2 + 1, 1])
            hit = row == order_ref[i : i + 1, :]
            ids = ids + jnp.where(hit, pair[0:1, :], jnp.float32(0.0))
            scale = scale + jnp.where(hit, pair[1:2, :], jnp.float32(0.0))
        r = pl.ds(pl.multiple_of(first, 128), 128)
        ids = jnp.broadcast_to(jnp.sum(ids, axis=1, keepdims=True), (128, 128))
        chb[r, :] = ids
        for c in range(4):
            kb[c, r, :] = jnp.where(ids == jnp.float32(c), jnp.float32(1.0), jnp.float32(0.0)).astype(BF)
        scb[r, :] = jnp.broadcast_to(jnp.sum(scale, axis=1, keepdims=True), (128, 128))

    own_copies[2].wait()
    acc[2] = raw(2)

    def mask_rows(g):
        @pl.loop(0, rows // 128)
        def _(m):
            r = pl.ds(pl.multiple_of(m * 128, 128), 128)
            for c in range(4):
                for kq in range(4):
                    v = out_ref[r, pl.ds(pl.multiple_of((kq * GK + g) * 128, 128), 128)]
                    tm[g, r, (c * 4 + kq) * 128 : (c * 4 + kq + 1) * 128] = v * kb[c, r, :]

    def finish_own():
        own_copies[3].wait()
        wide = raw(3)
        for m in range(rows // 128):
            r = slice(m * 128, (m + 1) * 128)
            ids, scale = chb[r, :], scb[r, :]
            for part in range(4):
                col = slice(part * 128, (part + 1) * 128)
                v = jnp.where(ids == jnp.float32(3), wide[r, col], jnp.float32(0.0))
                for c in range(3):
                    v = jnp.where(ids == jnp.float32(c), acc[c, r, col], v)
                out_ref[r, pl.ds(pl.multiple_of(z * 512 + part * 128, 128), 128)] = (v * scale).astype(BF)

    def unit(dq, g, slot):
        gk = g % GK
        nh = g // GK
        cols = pl.ds(pl.multiple_of(nh * NB, NB), NB)

        @pl.when(gk == 0)
        def _():
            acc[slot, :, cols] = jnp.zeros((rows, NB), F32)

        rhs = wbuf[pl.ds(((dq - 1) * G + g) * 16, 16)].reshape(2048, NB)
        acc[slot, :, cols] += jnp.dot(tm[gk], rhs, preferred_element_type=F32)

        @pl.when(gk == GK - 1)
        def _():
            first = ((z + dq) % NZ) * 512 + nh * NB

            @pl.loop(0, rows // 128)
            def _(m):
                r = pl.ds(pl.multiple_of(m * 128, 128), 128)
                for part in range(NB // 128):
                    src = pl.ds(pl.multiple_of(nh * NB + part * 128, 128), 128)
                    dst = pl.ds(pl.multiple_of(first + part * 128, 128), 128)
                    out_ref[r, dst] = (acc[slot, r, src] * scb[r, :]).astype(BF)


    def work(dq, g):
        arrive(spot(dq, g, 2 - 2 * core, 0), 0, 8)
        unit(dq, g, dq - 1)

    def step(s, carry):
        @pl.when(s + LEAD < steps)
        def _():
            first_arrivals(s + LEAD)

        @pl.when(s < steps)
        def _():
            for along_y, c, kq, plus, minus in ((0, cx, x, XP, XM), (1, cy, y, YP, YM)):
                dq, g = place(s, along_y)
                below, above = spot(dq, g, c, (kq + 3) % 4), spot(dq, g, c, (kq + 1) % 4)
                arrive(spot(dq, g, c, 0), 3 + along_y, 2)
                send(plus, wbuf.at[below, 0:64], below, 5 + along_y, (0, 64))
                send(minus, wbuf.at[above, 64:128], above, 5 + along_y, (64, 128))
                forward(SIB, below, 0)
                forward(SIB, above, 0)

        @pl.when(s == PURE)
        def _():
            for kq in range(4):
                for c in (cx, cy):
                    send_own(ZP, 3, c, kq, G - 1, 1 + kq)
                    send_own(ZM, 1, c, kq, G - 1, 1 + kq)

        @pl.when(jnp.logical_and(s >= PURE_IN, s < PURE_IN + 4))
        def _():
            kq = s - PURE_IN
            for dq in (3, 1):
                arrive(spot(dq, G - 1, 0, 0), 1 + kq, 2)
            send(ZP, wbuf.at[spot(3, G - 1, cx, kq)], spot(2, G - 1, cx, kq), 1 + kq)
            send(ZM, wbuf.at[spot(1, G - 1, cy, kq)], spot(2, G - 1, cy, kq), 1 + kq)
            for dq in (3, 1):
                for c in (cx, cy):
                    forward(SIB, spot(dq, G - 1, c, kq), 0)

        @pl.when(s < GK)
        def _():
            mask_rows(s)

        @pl.when(s == GK)
        def _():
            finish_own()

        @pl.when(s >= LD)
        def _():
            work(*place(s - LD, 0))

        @pl.when(jnp.logical_and(s >= steps, s < steps + 2))
        def _():
            work(3 - 2 * (s - steps), G - 1)

        @pl.when(jnp.logical_and(s >= LC, s < steps + LC))
        def _():
            for along_y, c, kq in ((0, cx, x), (1, cy, y)):
                dq, g = place(s - LC, along_y)
                index = spot(dq, g, c, (kq + 2) % 4)
                arrive(index, 5 + along_y)
                forward(SIB, index, 0)

        return carry

    lax.fori_loop(0, steps + LC, step, 0)

    for kq in range(4):
        arrive(spot(2, G - 1, 0, 0), 1 + kq, 2)
        for c in (cx, cy):
            forward(SIB, spot(2, G - 1, c, kq), 0)

    def rest(g, carry):
        work(2, g)
        return carry

    lax.fori_loop(ring - (LD - LC), G, rest, 0)

    for link in (XP, XM, YP, YM):
        whole = wbuf.at[pl.ds(0, steps * 3), 0:64]
        pltpu.make_async_copy(whole, whole, send_sem.at[link]).wait()
    for link, count in ((ZP, steps + 12), (ZM, steps + 12), (SIB, 3 * G * 8)):
        whole = wbuf.at[pl.ds(0, count)]
        pltpu.make_async_copy(whole, whole, send_sem.at[link]).wait()
    for one in tells:
        one.wait_send()


def slot_values(recv_order, ph_channel, recouple_weight, rows):
    start = lax.axis_index("int") * rows
    ids = lax.dynamic_slice(ph_channel, (start,), (rows,)).astype(F32)
    scale = lax.dynamic_slice(recouple_weight, (start,), (rows,))
    hit = recv_order[None, :] == jnp.arange(rows, dtype=jnp.int32)[:, None]
    both = [jnp.sum(jnp.where(hit, v[None, :], jnp.float32(0.0)), axis=1) for v in (ids, scale)]
    quota = rows // lax.axis_size("chan")
    lanes = jnp.stack(both).reshape(2, NX, NY, NCORE, quota).transpose(1, 2, 3, 0, 4)
    mine = (jnp.arange(128) // quota) == lax.axis_index("chan") % (128 // quota)
    return jnp.where(mine, jnp.tile(lanes, (1, 1, 1, 1, 128 // quota)), jnp.float32(0.0))


def on_device(t_pp, interaction, send_order, recv_order, ph_channel, recouple_weight):
    rows = t_pp.shape[0]
    meta = slot_values(recv_order, ph_channel, recouple_weight, rows)
    pieces = interaction.reshape(4, 4, GK, 128, 512)
    anyspace = pl.BlockSpec(memory_space=pl.ANY)
    vmem = pl.BlockSpec(memory_space=pltpu.VMEM)
    meta_shape = (NX, NY, NCORE, 2, 128)
    return pl.pallas_call(
        kernel,
        out_shape=pltpu.VMEM(t_pp.shape, BF),
        in_specs=[anyspace, anyspace, anyspace, vmem],
        out_specs=vmem,
        scratch_shapes=[
            pltpu.VMEM((4, 4, GK, 128, 512), BF),
            pltpu.VMEM((3 * G * 16, 128, NB), BF),
            pltpu.VMEM((GK, rows, 2048), BF),
            pltpu.VMEM((3, rows, 512), F32),
            pltpu.VMEM((rows, 128), F32),
            pltpu.VMEM((rows, 128), F32),
            pltpu.VMEM((4, rows, 128), BF),
            pltpu.VMEM(meta_shape, F32),
            pltpu.VMEM(meta_shape, F32),
            pltpu.VMEM(meta_shape, F32),
            pltpu.SemaphoreType.DMA((5,)),
            pltpu.SemaphoreType.DMA((7,)),
            pltpu.SemaphoreType.DMA((3 * G * KINDS,)),
            pltpu.SemaphoreType.DMA((10,)),
            pltpu.SemaphoreType.DMA((7,)),
        ],
        compiler_params=pltpu.CompilerParams(
            collective_id=0, has_side_effects=True, vmem_limit_bytes=62500000
        ),
    )(t_pp, pieces, meta, send_order.reshape(rows // 128, 128))


def solution(mesh):
    in_specs = (
        P(("chan", "int"), None),
        P(None, None, "int"),
        P(("chan", "int")),
        P(("chan", "int")),
        P("chan"),
        P("chan"),
    )
    out_specs = P(("chan", "int"), None)
    return jax.shard_map(
        on_device, mesh=mesh, in_specs=in_specs, out_specs=out_specs, check_vma=False
    )
```
